256 devices in a mesh: expert: 8 (over x, core), hidden: 32 (over y, z).
Axes of the slice: x: 4, y: 4, z: 8, core: 2. Of those that a mesh axis runs over, the one named last changes fastest.
Arguments:
- tokens: bfloat16 [1024, 6144], P(('expert', 'hidden')), may hold values from -33 to 33
- norm_gain: float32 [6144], replicated, may hold values from 0.1 to 1.9
- gate_weight: bfloat16 [8, 6144, 8192], P('expert', None, 'hidden'), may hold values from -0.078125 to 0.078125
- up_weight: bfloat16 [8, 6144, 8192], P('expert', None, 'hidden'), may hold values from -0.078125 to 0.078125
- down_weight: bfloat16 [8, 8192, 6144], P('expert', 'hidden'), may hold values from -0.125 to 0.125
- expert_ids: int32 [1024, 2], P('expert'), may hold values from 0 to 7, all different within a row; in each aligned block of 4 rows (0 to 3, 4 to 7, ...) at most 2 rows name the same one
- route_weight: float32 [1024, 2], P('expert'), may hold values from 0.2 to 1
Outputs:
- settled_state: bfloat16 [1024, 6144], P(('expert', 'hidden'))
The draws below stay inside these ranges and needn't reach their ends.
Inputs may be any that keep to these rules, and one draw needn't show every extreme that they name: `expert_ids`: in each aligned block of 4 rows (the tokens of one device) the two ids of a row differ and no expert is named more than 2 times; some expert is named exactly 2 times.
All inputs are finite; a program needn't handle non-finite values.
Results may differ from the reference program's by a relative error of at most 0.0085.
Values may be sent and summed in bfloat16 or wider, within the bound.
No kernel may reach another device: no remote copies, remote signals or barrier semaphores. Data moves between devices by JAX's collectives and lax.ppermute only.
A program may use at most 64 MiB of HBM per device.

```python
import math
import jax
import jax.numpy as jnp
import numpy as np
from jax import lax

D = 6144
FF = 8192
TOK_DEV = 4
ITERS = 2
EXPERTS = 8
CAP = 2
TOKENS = 1024
N_HIDDEN = 32


def draw_tokens(key, part):
    noise_key, row_key, column_key = jax.random.split(key, 3)
    row_scale = jnp.exp(jax.random.uniform(row_key, (TOKENS, 1), jnp.float32, math.log(0.25), math.log(2.5)))
    column_scale = jnp.exp(jax.random.uniform(column_key, (1, D), jnp.float32, math.log(0.25), math.log(2.5)))
    base = jnp.clip(jax.random.normal(noise_key, (TOKENS, D), jnp.float32), -4.0, 4.0)
    return (base * row_scale * column_scale).astype(jnp.bfloat16)


def spiked(result, own_key, source, target, shards_of, factor):
    owner, partner = [(jnp.arange(result.shape[axis_at]) // (result.shape[axis_at] // shards_of)).reshape([-1 if axis == axis_at else 1 for axis in range(result.ndim)]) for axis_at in (source, target)]
    chosen = jax.random.permutation(own_key, shards_of)[partner]
    strong = (owner == chosen) | (owner == (partner + shards_of // 2) % shards_of)
    return jnp.where(strong, factor * result, result)


def steps_of(rng, dims, pieces, least, high):
    def one(axis_at, blocks):
        heights = jax.random.uniform(jax.random.fold_in(jax.random.fold_in(rng, 6), axis_at), (blocks,), jnp.float32, least / len(pieces), high / len(pieces))
        return jnp.repeat(jnp.exp(heights), dims[axis_at] // blocks).reshape((-1,) + (1,) * (len(dims) - axis_at - 1))

    gain = one(*pieces[0])
    for cut in pieces[1:]:
        gain = gain * one(*cut)
    return gain


def routed_block(rng, own, number, rows, amount, top, limit, lean):
    sequence = jax.random.permutation(rng, amount)
    packed, usual = portions_of(amount, rows * top, limit, lean, True), portions_of(amount, rows * top, limit, lean, False)
    places = jnp.arange(amount)

    def named(tallies, turn):
        used = int((tallies > 0).sum())
        fixed = max(1, used // 4)
        shifted = fixed + (places - fixed + turn * (used - fixed)) % max(1, amount - fixed)
        return jnp.zeros((amount,), jnp.int32).at[sequence[jnp.where(places < fixed, places, shifted)]].set(jnp.asarray(tallies, jnp.int32))

    tallies = jnp.where(number % 4 == 0, named(packed, number // 4), named(usual, number - number // 4 - 1))
    mixed = jax.random.permutation(jax.random.fold_in(own, 3), amount)
    donor, receiver = mixed[0:amount // 2 * 2:2], mixed[1:amount // 2 * 2:2]
    room = jnp.minimum(tallies[donor] - 1, limit - tallies[receiver]) // 2
    room = jnp.where((donor == sequence[0]) | (receiver == sequence[0]) | (tallies[receiver] == 0), 0, jnp.maximum(room, 0))
    shifted = jax.random.randint(jax.random.fold_in(own, 4), (amount // 2,), 0, 1 << 20) % (room + 1)
    tallies = tallies.at[donor].add(-shifted).at[receiver].add(shifted)
    members = jnp.searchsorted(jnp.cumsum(tallies), jnp.arange(rows * top), side="right").astype(jnp.int32)
    table = members.reshape(top, rows).T
    table = table[jax.random.permutation(jax.random.fold_in(own, 1), rows)]
    turn = jax.random.randint(jax.random.fold_in(own, 2), (rows, 1), 0, top)
    return jnp.take_along_axis(table, (jnp.arange(top)[None, :] + turn) % top, axis=1)


def portions_of(amount, total, most, slope, full):
    portions = [(1 << 20) // math.isqrt(rank ** slope) + 1 for rank in range(1, amount + 1)]
    largest = most if full else min(most, max(-(-total // amount), total * portions[0] // sum(portions)))
    least = 1 if total - largest >= amount - 1 else 0
    holding, rest = [largest] + [least] * (amount - 1), total - largest - least * (amount - 1)
    while rest > 0:
        candidates = [i for i in range(1, amount) if holding[i] < largest] or [i for i in range(1, amount) if holding[i] < most]
        whole, budget = sum([portions[i] for i in candidates]), rest
        for i in candidates:
            more = min(most - holding[i], max(1, budget * portions[i] // whole), rest)
            holding[i] = holding[i] + more
            rest = rest - more
    return np.array(holding)


def scatter_about(key, extent, deviation, bound, cuts=(), held_as=jnp.bfloat16):
    entries = deviation * jax.random.normal(key, extent, jnp.float32)
    if cuts:
        entries = entries * steps_of(key, extent, cuts, -0.22, 0.18)
    return jnp.clip(entries, -bound, bound).astype(held_as)


def bell_draw_with(stream_key, shape, deviation, limit, shards, heavy, held_as=jnp.bfloat16):
    entries = deviation * jax.random.normal(stream_key, shape, jnp.float32)
    if shards:
        entries = entries * steps_of(stream_key, shape, shards, -0.22, 0.18)
    return jnp.clip(spiked(entries, jax.random.fold_in(stream_key, 3), *heavy), -limit, limit).astype(held_as)


def setup_inputs(seed: int = 0) -> dict:
    seeds = jax.random.split(jax.random.key(seed), 8)
    tokens = draw_tokens(jax.random.fold_in(seeds[7], 71), 0)
    norm_gain = jnp.clip(1.0 + 0.18 * jax.random.normal(seeds[1], (D,), jnp.float32), 0.1, 1.9)
    gate_weight = scatter_about(seeds[2], (EXPERTS, D, FF), D ** -0.5, 0.078125, ((0, 8), (2, 32)))
    up_weight = scatter_about(seeds[3], (EXPERTS, D, FF), D ** -0.5, 0.078125, ((0, 8), (2, 32)))
    down_weight = bell_draw_with(seeds[4], (EXPERTS, FF, D), FF ** -0.5, 0.125, ((0, 8), (1, 32)), (1, 2, 32, 2.75))
    expert_ids_keys = jax.random.split(jax.random.fold_in(seeds[5], 1), TOKENS // TOK_DEV)
    expert_ids_turns = jax.random.permutation(jax.random.fold_in(seeds[5], 3), TOKENS // TOK_DEV)
    expert_ids = jax.vmap(lambda own, number: routed_block(jax.random.fold_in(seeds[5], 2), own, number, TOK_DEV, EXPERTS, 2, CAP, 2))(expert_ids_keys, expert_ids_turns).reshape((TOKENS, 2))
    route_weight = jnp.clip(0.2 + 0.8 * jax.random.uniform(seeds[6], (TOKENS, 2), jnp.float32) ** steps_of(seeds[6], (TOKENS, 2), ((0, 8),), -0.2, 0.2), 0.2, 1.0)
    return dict(tokens=tokens, norm_gain=norm_gain, gate_weight=gate_weight, up_weight=up_weight, down_weight=down_weight, expert_ids=expert_ids, route_weight=route_weight)


EPSILON = 1e-05
NUDGE = 0.5

def rms_norm(values, norm_gain):
    widened = values.astype(jnp.float32)
    mean_square = lax.optimization_barrier(jnp.mean(widened * widened, axis=-1, keepdims=True))
    return (widened * lax.rsqrt(mean_square + EPSILON) * norm_gain).astype(jnp.bfloat16)

def expert_outputs(normed, gate_panel, up_panel, down_panel, chosen):
    inputs = jnp.take(normed, chosen, axis=0)
    gate_value = jnp.dot(inputs, gate_panel, preferred_element_type=jnp.float32)
    up_value = jnp.dot(inputs, up_panel, preferred_element_type=jnp.float32)
    hidden_units = (jax.nn.silu(gate_value) * up_value).astype(jnp.bfloat16)
    unit_block = FF // N_HIDDEN

    def add_block(block_index, total):
        start = (block_index * unit_block).astype(jnp.int32)
        units = lax.dynamic_slice_in_dim(hidden_units, start, unit_block, 1)
        panel = lax.dynamic_slice_in_dim(down_panel, start, unit_block, 0)
        partial_sum = jnp.dot(units, panel, preferred_element_type=jnp.float32).astype(jnp.bfloat16)
        partial_sum = lax.optimization_barrier(partial_sum)
        return total + partial_sum.astype(jnp.float32)
    total = lax.fori_loop(0, N_HIDDEN, add_block, jnp.zeros((chosen.shape[0], D), jnp.float32))
    return total.astype(jnp.bfloat16)

def reference(tokens, norm_gain, gate_weight, up_weight, down_weight, expert_ids, route_weight):
    state = tokens
    token_index = jnp.arange(TOKENS, dtype=jnp.int32)
    for iteration in range(ITERS):
        normed = rms_norm(state, norm_gain)

        def one_expert(expert):
            routed = jnp.any(expert_ids == expert, axis=1)
            order_keys = jnp.where(routed, 0, 1).astype(jnp.int32)
            chosen = jnp.argsort(order_keys, stable=True)[:TOKENS // 2].astype(jnp.int32)
            values = expert_outputs(normed, gate_weight[expert], up_weight[expert], down_weight[expert], chosen)
            return jnp.zeros((TOKENS, D), jnp.bfloat16).at[chosen].set(values)
        outputs = lax.map(one_expert, jnp.arange(EXPERTS, dtype=jnp.int32))
        first = outputs[expert_ids[:, 0], token_index].astype(jnp.float32) * route_weight[:, 0:1]
        second = outputs[expert_ids[:, 1], token_index].astype(jnp.float32) * route_weight[:, 1:2]
        mixed = first + second
        state = (NUDGE * state.astype(jnp.float32) + NUDGE * (tokens.astype(jnp.float32) + mixed)).astype(jnp.bfloat16)
    return state
```

```python
import jax
import jax.numpy as jnp
from jax import lax
from jax.experimental import pallas as pl
from jax.experimental.pallas import tpu as pltpu
from jax.sharding import PartitionSpec as P

ITERS = 2
EPSILON = 1e-05
NUDGE = 0.5
RING = 4

BF16 = jnp.bfloat16
F32 = jnp.float32


def row_groups(hidden):
    depth = hidden // RING
    across = [[y * depth + z for y in range(RING)] for z in range(depth)]
    along = [[y * depth + z for z in range(depth)] for y in range(RING)]
    return across, along


def home_groups(experts, hidden):
    depth = hidden // RING
    return [
        [e * hidden + y * depth + z for e in range(experts) for y in range(RING)]
        for z in range(depth)
    ]


def rms_norm(values, norm_gain):
    widened = values.astype(F32)
    mean_square = jnp.mean(widened * widened, axis=-1, keepdims=True)
    return (widened * lax.rsqrt(mean_square + EPSILON) * norm_gain).astype(BF16)


def routing(ids, weights, slot_count, capacity):
    tok_count = ids.shape[0]
    flat = ids.reshape(-1)
    order = jnp.arange(flat.shape[0], dtype=jnp.int32)
    earlier = (flat[:, None] == flat[None, :]) & (order[None, :] < order[:, None])
    within = jnp.sum(earlier.astype(jnp.int32), axis=1)
    slots = (flat * capacity + within).reshape(tok_count, 2)
    hits = slots[:, :, None] == jnp.arange(slot_count, dtype=jnp.int32)[None, None, :]
    send = jnp.sum(hits.astype(F32), axis=1).astype(BF16)
    mix = jnp.sum(jnp.where(hits, weights[:, :, None], 0.0), axis=1)
    return send, mix


def exchange(values, axis, groups):
    return lax.all_to_all(values, axis, 0, 0, tiled=True, axis_index_groups=groups)


def spread(values, copies, axis, groups):
    return exchange(jnp.broadcast_to(values[None], (copies,) + values.shape), axis, groups)


def shifts(hidden, step, ring):
    depth = hidden // RING
    if ring == "along":
        return [(i, (i // depth) * depth + (i % depth + step) % depth) for i in range(hidden)]
    return [(i, ((i // depth + step) % RING) * depth + i % depth) for i in range(hidden)]


def shift(values, hidden, step, ring):
    return lax.ppermute(values, "hidden", shifts(hidden, step, ring))


def ring_gather(own, hidden):
    half = own.shape[0] // 2
    up, down = own, own
    blocks = {0: own}
    for step in range(1, 4):
        up, down = shift(up, hidden, 1, "along"), shift(down, hidden, -1, "along")
        blocks[-step], blocks[step] = up, down
    blocks[4] = jnp.concatenate(
        [shift(up[:half], hidden, 1, "along"), shift(down[half:], hidden, -1, "along")]
    )
    return blocks


def ring_sum(blocks, far, hidden, ring):
    half = blocks[0].shape[0] // 2
    wide = {k: v.astype(F32) for k, v in blocks.items()}
    up = shift(blocks[far][:half], hidden, 1, ring).astype(F32)
    down = shift(blocks[far][half:], hidden, -1, ring).astype(F32)
    for step in range(far - 1, 0, -1):
        right, left = wide[step], wide[-step]
        if step == far - 1:
            right = jnp.concatenate([right[:half] + up, right[half:]])
            left = jnp.concatenate([left[:half], left[half:] + down])
        else:
            right, left = right + up, left + down
        up = shift(right.astype(BF16), hidden, 1, ring).astype(F32)
        down = shift(left.astype(BF16), hidden, -1, ring).astype(F32)
    return wide[0] + up + down


def feature_part(weight, position, hidden, step):
    depth = hidden // RING
    part = weight.shape[0] // RING
    start = lax.rem(position // depth + step, RING) * part
    rows = lax.dynamic_slice_in_dim(weight, start, part, 0)
    return shift(rows, hidden, step, "across") if step else rows


def hold(values):
    return pltpu.with_memory_space_constraint(values, pltpu.HBM)


def whole_block():
    return pl.BlockSpec(memory_space=pltpu.VMEM)


def params(mib):
    return pltpu.CompilerParams(
        dimension_semantics=("arbitrary",), vmem_limit_bytes=mib * 1024 * 1024
    )


def silu_product(gate_value, up_value):
    return (gate_value / (1.0 + jnp.exp(-gate_value)) * up_value).astype(BF16)


def whole_gate_up(rows, gate, up):
    count, width = rows.shape
    units = gate.shape[1]
    depth = width // 6

    def kernel(rows_ref, gate_ref, up_ref, out_ref, gate_sum, up_sum):
        step = pl.program_id(0)
        block = rows_ref[...]
        features = pl.ds(pl.multiple_of(step * depth, depth), depth)
        gate_part = jnp.dot(block, gate_ref[features, :], preferred_element_type=F32)
        up_part = jnp.dot(block, up_ref[features, :], preferred_element_type=F32)

        @pl.when(step == 0)
        def _():
            gate_sum[...] = gate_part
            up_sum[...] = up_part

        @pl.when(step > 0)
        def _():
            gate_sum[...] += gate_part
            up_sum[...] += up_part

        @pl.when(step == pl.num_programs(0) - 1)
        def _():
            out_ref[...] = silu_product(gate_sum[...], up_sum[...])

    return pl.pallas_call(
        kernel,
        grid=(width // depth,),
        in_specs=[
            pl.BlockSpec((count, depth), lambda k: (0, k)),
            whole_block(),
            whole_block(),
        ],
        out_specs=pl.BlockSpec((count, units), lambda k: (0, 0)),
        out_shape=jax.ShapeDtypeStruct((count, units), BF16),
        scratch_shapes=[pltpu.VMEM((count, units), F32), pltpu.VMEM((count, units), F32)],
        compiler_params=params(24),
        cost_estimate=pl.CostEstimate(
            flops=4 * count * width * units,
            bytes_accessed=2 * (count * width + 2 * width * units),
            transcendentals=count * units,
        ),
    )(hold(rows), gate, up)


def part_gate_up(rows, gate, up_parts, place):
    count, part = rows.shape
    units = gate.shape[1]

    def kernel(place_ref, rows_ref, gate_ref, up_ref, out_ref):
        block = rows_ref[...]
        out_ref[:, :units] = jnp.dot(block, gate_ref[...], preferred_element_type=F32).astype(BF16)
        up = up_ref[place_ref[0]]
        out_ref[:, units:] = jnp.dot(block, up, preferred_element_type=F32).astype(BF16)

    return pl.pallas_call(
        kernel,
        in_specs=[pl.BlockSpec(memory_space=pltpu.SMEM)] + [whole_block()] * 3,
        out_specs=whole_block(),
        out_shape=jax.ShapeDtypeStruct((count, 2 * units), BF16),
        compiler_params=pltpu.CompilerParams(vmem_limit_bytes=8 * 1024 * 1024),
        cost_estimate=pl.CostEstimate(
            flops=4 * count * part * units,
            bytes_accessed=2 * (count * part + 2 * part * units + count * units * 2),
            transcendentals=0,
        ),
    )(place, rows, gate, up_parts)


def down_product(gathered, down_parts):
    ring, count, units = gathered.shape
    part = down_parts.shape[2]
    columns = part // 3

    def kernel(rows_ref, down_ref, out_ref):
        total = jnp.dot(rows_ref[0], down_ref[0], preferred_element_type=F32)
        for y in range(1, ring):
            total = total + jnp.dot(rows_ref[y], down_ref[y], preferred_element_type=F32)
        out_ref[...] = total.astype(BF16)

    return pl.pallas_call(
        kernel,
        grid=(part // columns,),
        in_specs=[whole_block(), pl.BlockSpec((ring, units, columns), lambda n: (0, 0, n))],
        out_specs=pl.BlockSpec((count, columns), lambda n: (0, n)),
        out_shape=jax.ShapeDtypeStruct((count, part), BF16),
        compiler_params=params(16),
        cost_estimate=pl.CostEstimate(
            flops=2 * count * part * units * ring,
            bytes_accessed=2 * (ring * count * units + ring * units * part + count * part),
            transcendentals=0,
        ),
    )(gathered, down_parts)


def on_device(tokens, norm_gain, gate_weight, up_weight, down_weight, expert_ids, route_weight):
    experts = lax.axis_size("expert")
    hidden = lax.axis_size("hidden")
    depth = hidden // RING
    tok_count, width = tokens.shape
    part = width // RING
    units = gate_weight.shape[2]
    capacity = tok_count // 2
    slot_count = experts * capacity
    block = RING * slot_count
    across, along = row_groups(hidden)
    homes = home_groups(experts, hidden)
    both = ("expert", "hidden")

    position = lax.axis_index("hidden")
    own_ids = lax.dynamic_slice_in_dim(expert_ids, position * tok_count, tok_count, 0)
    own_weights = lax.dynamic_slice_in_dim(route_weight, position * tok_count, tok_count, 0)
    send, mix = routing(own_ids, own_weights, slot_count, capacity)

    def outgoing(state):
        normed = rms_norm(state, norm_gain)
        return jnp.einsum("ts,td->sd", send, normed, preferred_element_type=F32).astype(BF16)

    def finish(units_of, down_parts):
        return down_product(spread(units_of, RING, "hidden", across), down_parts)

    def settle(summed, state):
        returned = exchange(summed.astype(BF16).reshape(experts * RING, capacity, part), both, homes)
        returned = returned.reshape(experts, RING, capacity, part).astype(F32)
        mixed = jnp.einsum(
            "tec,eycd->tyd",
            mix.reshape(tok_count, experts, capacity),
            returned,
            precision=lax.Precision.HIGHEST,
        ).reshape(tok_count, width)
        return (
            NUDGE * state.astype(F32) + NUDGE * (tokens.astype(F32) + mixed)
        ).astype(BF16)

    rows = outgoing(tokens).reshape(experts, 1, capacity, width)
    rows = jnp.broadcast_to(rows, (experts, RING, capacity, width))
    rows = exchange(rows.reshape(experts * RING, capacity, width), both, homes)
    rows = rows.reshape(block, width)
    gate, up, down = gate_weight[0], up_weight[0], down_weight[0]
    near = [feature_part(gate, position, hidden, step) for step in (1, 3)]
    rows, down_in = lax.optimization_barrier((rows, down))
    gathered = lax.all_gather(rows, "hidden", axis=0, tiled=True, axis_index_groups=along)
    down_parts = exchange(
        down_in.reshape(units, RING, part).transpose(1, 0, 2), "hidden", across
    )
    gathered, near, down_parts = lax.optimization_barrier((gathered, near, down_parts))
    partial = finish(whole_gate_up(gathered, gate, up), down_parts)
    partial, up_in = lax.optimization_barrier((partial, up))
    up_parts = [feature_part(up_in, position, hidden, step) for step in range(RING)]
    summed = lax.psum_scatter(
        partial, "hidden", scatter_dimension=0, tiled=True, axis_index_groups=along
    )
    up_parts = exchange(up_in.reshape(RING, part, units), "hidden", across)
    summed, up_parts = lax.optimization_barrier((summed, up_parts))
    state = settle(summed, tokens)

    rows = outgoing(state).reshape(experts, capacity, RING, part).transpose(0, 2, 1, 3)
    rows = exchange(rows.reshape(experts * RING, capacity, part), both, homes)
    rows, gate_in = lax.optimization_barrier((rows, gate))
    far = [feature_part(gate_in, position, hidden, step) for step in (0, 2)]
    gate_parts = [far[0], near[0], far[1], near[1]]
    blocks = ring_gather(rows.reshape(block, part), hidden)
    offsets = sorted(blocks)
    gathered = jnp.concatenate([blocks[step] for step in offsets])
    gathered, gate_parts = lax.optimization_barrier((gathered, gate_parts))
    values = {
        step: part_gate_up(
            gathered,
            gate_parts[-step % RING],
            up_parts,
            lax.rem(position // depth + step + RING, RING).reshape(1),
        )
        for step in (2, 1, -1, 0)
    }
    values = ring_sum(values, 2, hidden, "across")
    partial = finish(silu_product(values[:, :units], values[:, units:]), down_parts)
    blocks = {
        step: partial[place * block : (place + 1) * block] for place, step in enumerate(offsets)
    }
    return settle(ring_sum(blocks, 4, hidden, "along"), state)


def solution(mesh):
    placed = (
        P(("expert", "hidden"), None),
        P(),
        P("expert", None, "hidden"),
        P("expert", None, "hidden"),
        P("expert", "hidden", None),
        P("expert", None),
        P("expert", None),
    )
    return jax.shard_map(
        on_device,
        mesh=mesh,
        in_specs=placed,
        out_specs=P(("expert", "hidden"), None),
        check_vma=False,
    )
```

```python
import jax
import jax.numpy as jnp
from jax import lax
from jax.experimental import pallas as pl
from jax.experimental.pallas import tpu as pltpu
from jax.sharding import PartitionSpec as P

ITERS = 2
EPSILON = 1e-05
NUDGE = 0.5
RING = 4

BF16 = jnp.bfloat16
F32 = jnp.float32


def row_groups(hidden):
    depth = hidden // RING
    across = [[y * depth + z for y in range(RING)] for z in range(depth)]
    along = [[y * depth + z for z in range(depth)] for y in range(RING)]
    return across, along


def home_groups(experts, hidden):
    depth = hidden // RING
    return [
        [e * hidden + y * depth + z for e in range(experts) for y in range(RING)]
        for z in range(depth)
    ]


def rms_norm(values, norm_gain):
    widened = values.astype(F32)
    mean_square = jnp.mean(widened * widened, axis=-1, keepdims=True)
    return (widened * lax.rsqrt(mean_square + EPSILON) * norm_gain).astype(BF16)


def routing(ids, weights, slot_count, capacity):
    tok_count = ids.shape[0]
    flat = ids.reshape(-1)
    order = jnp.arange(flat.shape[0], dtype=jnp.int32)
    earlier = (flat[:, None] == flat[None, :]) & (order[None, :] < order[:, None])
    within = jnp.sum(earlier.astype(jnp.int32), axis=1)
    slots = (flat * capacity + within).reshape(tok_count, 2)
    hits = slots[:, :, None] == jnp.arange(slot_count, dtype=jnp.int32)[None, None, :]
    send = jnp.sum(hits.astype(F32), axis=1).astype(BF16)
    mix = jnp.sum(jnp.where(hits, weights[:, :, None], 0.0), axis=1)
    return send, mix


def exchange(values, axis, groups):
    return lax.all_to_all(values, axis, 0, 0, tiled=True, axis_index_groups=groups)


def spread(values, copies, axis, groups):
    return exchange(jnp.broadcast_to(values[None], (copies,) + values.shape), axis, groups)


def shifts(hidden, step, ring):
    depth = hidden // RING
    if ring == "along":
        return [(i, (i // depth) * depth + (i % depth + step) % depth) for i in range(hidden)]
    return [(i, ((i // depth + step) % RING) * depth + i % depth) for i in range(hidden)]


def shift(values, hidden, step, ring):
    return lax.ppermute(values, "hidden", shifts(hidden, step, ring))


def ring_gather(own, hidden):
    half = own.shape[0] // 2
    up, down = own, own
    blocks = {0: own}
    for step in range(1, 4):
        up, down = shift(up, hidden, 1, "along"), shift(down, hidden, -1, "along")
        blocks[-step], blocks[step] = up, down
    blocks[4] = jnp.concatenate(
        [shift(up[:half], hidden, 1, "along"), shift(down[half:], hidden, -1, "along")]
    )
    return blocks


def ring_sum(blocks, far, hidden, ring):
    half = blocks[0].shape[0] // 2
    wide = {k: v.astype(F32) for k, v in blocks.items()}
    up = shift(blocks[far][:half], hidden, 1, ring).astype(F32)
    down = shift(blocks[far][half:], hidden, -1, ring).astype(F32)
    for step in range(far - 1, 0, -1):
        right, left = wide[step], wide[-step]
        if step == far - 1:
            right = jnp.concatenate([right[:half] + up, right[half:]])
            left = jnp.concatenate([left[:half], left[half:] + down])
        else:
            right, left = right + up, left + down
        up = shift(right.astype(BF16), hidden, 1, ring).astype(F32)
        down = shift(left.astype(BF16), hidden, -1, ring).astype(F32)
    return wide[0] + up + down


def feature_part(weight, position, hidden, step, first=0, last=1, of=1):
    depth = hidden // RING
    part = weight.shape[0] // RING
    piece = part // of
    start = lax.rem(position // depth + step, RING) * part + first * piece
    rows = lax.dynamic_slice_in_dim(weight, start, (last - first) * piece, 0)
    return shift(rows, hidden, step, "across") if step else rows


def hold(values):
    return pltpu.with_memory_space_constraint(values, pltpu.HBM)


def whole_block():
    return pl.BlockSpec(memory_space=pltpu.VMEM)


def params(mib):
    return pltpu.CompilerParams(
        dimension_semantics=("arbitrary",), vmem_limit_bytes=mib * 1024 * 1024
    )


def silu_product(gate_value, up_value):
    return (gate_value / (1.0 + jnp.exp(-gate_value)) * up_value).astype(BF16)


def whole_gate_up(rows, gate, up):
    count, width = rows.shape
    units = gate.shape[1]
    pieces = 6
    depth = width // pieces

    def kernel(rows_hbm, gate_hbm, up_hbm, out_ref, rows_ref, gate_ref, up_ref, sems):
        copies = []
        for piece in range(pieces):
            features = pl.ds(piece * depth, depth)
            moved = [
                pltpu.make_async_copy(
                    rows_hbm.at[:, features], rows_ref.at[piece], sems.at[piece, 0]
                ),
                pltpu.make_async_copy(gate_hbm.at[features], gate_ref.at[piece], sems.at[piece, 1]),
                pltpu.make_async_copy(up_hbm.at[features], up_ref.at[piece], sems.at[piece, 2]),
            ]
            for copy in moved:
                copy.start()
            copies.append(moved)
        for copy in copies[0]:
            copy.wait()
        gate_sum = jnp.dot(rows_ref[0], gate_ref[0], preferred_element_type=F32)
        up_sum = jnp.dot(rows_ref[0], up_ref[0], preferred_element_type=F32)
        for piece in range(1, pieces):
            for copy in copies[piece]:
                copy.wait()
            gate_sum += jnp.dot(rows_ref[piece], gate_ref[piece], preferred_element_type=F32)
            up_sum += jnp.dot(rows_ref[piece], up_ref[piece], preferred_element_type=F32)
        out_ref[...] = silu_product(gate_sum, up_sum)

    anywhere = pl.BlockSpec(memory_space=pl.ANY)
    return pl.pallas_call(
        kernel,
        in_specs=[anywhere, anywhere, anywhere],
        out_specs=whole_block(),
        out_shape=jax.ShapeDtypeStruct((count, units), BF16),
        scratch_shapes=[
            pltpu.VMEM((pieces, count, depth), BF16),
            pltpu.VMEM((pieces, depth, units), BF16),
            pltpu.VMEM((pieces, depth, units), BF16),
            pltpu.SemaphoreType.DMA((pieces, 3)),
        ],
        compiler_params=pltpu.CompilerParams(vmem_limit_bytes=32 * 1024 * 1024),
        cost_estimate=pl.CostEstimate(
            flops=4 * count * width * units,
            bytes_accessed=2 * (count * width + 2 * width * units),
            transcendentals=count * units,
        ),
    )(hold(rows), hold(gate), hold(up))


def feature_blocks(weight):
    units, width = weight.shape
    part = width // RING

    def kernel(weight_hbm, out_ref, sems):
        moved = [
            pltpu.make_async_copy(
                weight_hbm.at[:, pl.ds(y * part, part)], out_ref.at[y], sems.at[y]
            )
            for y in range(RING)
        ]
        for copy in moved:
            copy.start()
        for copy in moved:
            copy.wait()

    return pl.pallas_call(
        kernel,
        in_specs=[pl.BlockSpec(memory_space=pl.ANY)],
        out_specs=whole_block(),
        out_shape=jax.ShapeDtypeStruct((RING, units, part), BF16),
        scratch_shapes=[pltpu.SemaphoreType.DMA((RING,))],
        compiler_params=pltpu.CompilerParams(vmem_limit_bytes=4 * 1024 * 1024),
        cost_estimate=pl.CostEstimate(
            flops=0, bytes_accessed=4 * units * width, transcendentals=0
        ),
    )(hold(weight))


def part_gate_up(rows, gate, up_parts, place):
    count, part = rows.shape
    units = gate.shape[1]

    def kernel(place_ref, rows_ref, gate_ref, up_ref, out_ref):
        block = rows_ref[...]
        out_ref[:, :units] = jnp.dot(block, gate_ref[...], preferred_element_type=F32).astype(BF16)
        up = up_ref[place_ref[0]]
        out_ref[:, units:] = jnp.dot(block, up, preferred_element_type=F32).astype(BF16)

    return pl.pallas_call(
        kernel,
        in_specs=[pl.BlockSpec(memory_space=pltpu.SMEM)] + [whole_block()] * 3,
        out_specs=whole_block(),
        out_shape=jax.ShapeDtypeStruct((count, 2 * units), BF16),
        compiler_params=pltpu.CompilerParams(vmem_limit_bytes=8 * 1024 * 1024),
        cost_estimate=pl.CostEstimate(
            flops=4 * count * part * units,
            bytes_accessed=2 * (count * part + 2 * part * units + count * units * 2),
            transcendentals=0,
        ),
    )(place, rows, gate, up_parts)


def down_product(gathered, down_parts):
    ring, count, units = gathered.shape
    part = down_parts.shape[2]
    columns = part // 3

    def kernel(rows_ref, down_ref, out_ref):
        total = jnp.dot(rows_ref[0], down_ref[0], preferred_element_type=F32)
        for y in range(1, ring):
            total = total + jnp.dot(rows_ref[y], down_ref[y], preferred_element_type=F32)
        out_ref[...] = total.astype(BF16)

    return pl.pallas_call(
        kernel,
        grid=(part // columns,),
        in_specs=[whole_block(), pl.BlockSpec((ring, units, columns), lambda n: (0, 0, n))],
        out_specs=pl.BlockSpec((count, columns), lambda n: (0, n)),
        out_shape=jax.ShapeDtypeStruct((count, part), BF16),
        compiler_params=params(16),
        cost_estimate=pl.CostEstimate(
            flops=2 * count * part * units * ring,
            bytes_accessed=2 * (ring * count * units + ring * units * part + count * part),
            transcendentals=0,
        ),
    )(gathered, down_parts)


def on_device(tokens, norm_gain, gate_weight, up_weight, down_weight, expert_ids, route_weight):
    experts = lax.axis_size("expert")
    hidden = lax.axis_size("hidden")
    depth = hidden // RING
    tok_count, width = tokens.shape
    part = width // RING
    units = gate_weight.shape[2]
    capacity = tok_count // 2
    slot_count = experts * capacity
    block = RING * slot_count
    across, along = row_groups(hidden)
    homes = home_groups(experts, hidden)
    both = ("expert", "hidden")

    position = lax.axis_index("hidden")
    own_ids = lax.dynamic_slice_in_dim(expert_ids, position * tok_count, tok_count, 0)
    own_weights = lax.dynamic_slice_in_dim(route_weight, position * tok_count, tok_count, 0)
    send, mix = routing(own_ids, own_weights, slot_count, capacity)

    def outgoing(state):
        normed = rms_norm(state, norm_gain)
        return jnp.einsum("ts,td->sd", send, normed, preferred_element_type=F32).astype(BF16)

    def finish(units_of, down_parts):
        return down_product(spread(units_of, RING, "hidden", across), down_parts)

    def settle(summed, state):
        returned = exchange(summed.astype(BF16).reshape(experts * RING, capacity, part), both, homes)
        returned = returned.reshape(experts, RING, capacity, part).astype(F32)
        mixed = jnp.einsum(
            "tec,eycd->tyd",
            mix.reshape(tok_count, experts, capacity),
            returned,
            precision=lax.Precision.HIGHEST,
        ).reshape(tok_count, width)
        return (
            NUDGE * state.astype(F32) + NUDGE * (tokens.astype(F32) + mixed)
        ).astype(BF16)

    rows = outgoing(tokens).reshape(experts, 1, capacity, width)
    rows = jnp.broadcast_to(rows, (experts, RING, capacity, width))
    rows = exchange(rows.reshape(experts * RING, capacity, width), both, homes)
    rows = rows.reshape(block, width)
    gate, up, down = gate_weight[0], up_weight[0], down_weight[0]
    near = [feature_part(gate, position, hidden, step) for step in (1, 3)]
    near.append(feature_part(gate, position, hidden, 2, 0, 1, 2))
    gathered = lax.all_gather(rows, "hidden", axis=0, tiled=True, axis_index_groups=along)
    down_parts = exchange(feature_blocks(down), "hidden", across)
    gathered, near, down_parts = lax.optimization_barrier((gathered, near, down_parts))
    partial = finish(whole_gate_up(gathered, gate, up), down_parts)
    partial, up_in = lax.optimization_barrier((partial, up))
    up_parts = [feature_part(up_in, position, hidden, step) for step in range(RING)]
    summed = lax.psum_scatter(
        partial, "hidden", scatter_dimension=0, tiled=True, axis_index_groups=along
    )
    up_parts = exchange(up_in.reshape(RING, part, units), "hidden", across)
    summed, up_parts = lax.optimization_barrier((summed, up_parts))
    state = settle(summed, tokens)

    rows = outgoing(state).reshape(experts, capacity, RING, part).transpose(0, 2, 1, 3)
    rows = exchange(rows.reshape(experts * RING, capacity, part), both, homes)
    rows, gate_in = lax.optimization_barrier((rows, gate))
    far = feature_part(gate_in, position, hidden, 2, 1, 2, 2)
    blocks = ring_gather(rows.reshape(block, part), hidden)
    offsets = sorted(blocks)
    gathered = jnp.concatenate([blocks[step] for step in offsets])
    gathered, far = lax.optimization_barrier((gathered, far))
    own = feature_part(gate, position, hidden, 0)
    gate_parts = [own, near[0], jnp.concatenate([near[2], far]), near[1]]
    values = {
        step: part_gate_up(
            gathered,
            gate_parts[-step % RING],
            up_parts,
            lax.rem(position // depth + step + RING, RING).reshape(1),
        )
        for step in (2, 1, -1, 0)
    }
    values = ring_sum(values, 2, hidden, "across")
    partial = finish(silu_product(values[:, :units], values[:, units:]), down_parts)
    blocks = {
        step: partial[place * block : (place + 1) * block] for place, step in enumerate(offsets)
    }
    return settle(ring_sum(blocks, 4, hidden, "along"), state)


def solution(mesh):
    placed = (
        P(("expert", "hidden"), None),
        P(),
        P("expert", None, "hidden"),
        P("expert", None, "hidden"),
        P("expert", "hidden", None),
        P("expert", None),
        P("expert", None),
    )
    return jax.shard_map(
        on_device,
        mesh=mesh,
        in_specs=placed,
        out_specs=P(("expert", "hidden"), None),
        check_vma=False,
    )
```

```python
import jax
import jax.numpy as jnp
from jax import lax
from jax.experimental import pallas as pl
from jax.experimental.pallas import tpu as pltpu
from jax.sharding import PartitionSpec as P

ITERS = 2
EPSILON = 1e-05
NUDGE = 0.5
RING = 4

BF16 = jnp.bfloat16
F32 = jnp.float32


def row_groups(hidden):
    depth = hidden // RING
    across = [[y * depth + z for y in range(RING)] for z in range(depth)]
    along = [[y * depth + z for z in range(depth)] for y in range(RING)]
    return across, along


def home_groups(experts, hidden):
    depth = hidden // RING
    return [
        [e * hidden + y * depth + z for e in range(experts) for y in range(RING)]
        for z in range(depth)
    ]


def rms_norm(values, norm_gain):
    widened = values.astype(F32)
    mean_square = jnp.mean(widened * widened, axis=-1, keepdims=True)
    return (widened * lax.rsqrt(mean_square + EPSILON) * norm_gain).astype(BF16)


def routing(ids, weights, slot_count, capacity):
    tok_count = ids.shape[0]
    flat = ids.reshape(-1)
    order = jnp.arange(flat.shape[0], dtype=jnp.int32)
    earlier = (flat[:, None] == flat[None, :]) & (order[None, :] < order[:, None])
    within = jnp.sum(earlier.astype(jnp.int32), axis=1)
    slots = (flat * capacity + within).reshape(tok_count, 2)
    hits = slots[:, :, None] == jnp.arange(slot_count, dtype=jnp.int32)[None, None, :]
    send = jnp.sum(hits.astype(F32), axis=1).astype(BF16)
    mix = jnp.sum(jnp.where(hits, weights[:, :, None], 0.0), axis=1)
    return send, mix


def exchange(values, axis, groups):
    return lax.all_to_all(values, axis, 0, 0, tiled=True, axis_index_groups=groups)


def spread(values, copies, axis, groups):
    return exchange(jnp.broadcast_to(values[None], (copies,) + values.shape), axis, groups)


def shifts(hidden, step, ring):
    depth = hidden // RING
    if ring == "along":
        return [(i, (i // depth) * depth + (i % depth + step) % depth) for i in range(hidden)]
    return [(i, ((i // depth + step) % RING) * depth + i % depth) for i in range(hidden)]


def shift(values, hidden, step, ring):
    return lax.ppermute(values, "hidden", shifts(hidden, step, ring))


def ring_gather(own, hidden):
    half = own.shape[0] // 2
    up, down = own, own
    blocks = {0: own}
    for step in range(1, 4):
        up, down = shift(up, hidden, 1, "along"), shift(down, hidden, -1, "along")
        blocks[-step], blocks[step] = up, down
    blocks[4] = jnp.concatenate(
        [shift(up[:half], hidden, 1, "along"), shift(down[half:], hidden, -1, "along")]
    )
    return blocks


def ring_sum(blocks, far, hidden, ring):
    half = blocks[0].shape[0] // 2
    wide = {k: v.astype(F32) for k, v in blocks.items()}
    up = shift(blocks[far][:half], hidden, 1, ring).astype(F32)
    down = shift(blocks[far][half:], hidden, -1, ring).astype(F32)
    for step in range(far - 1, 0, -1):
        right, left = wide[step], wide[-step]
        if step == far - 1:
            right = jnp.concatenate([right[:half] + up, right[half:]])
            left = jnp.concatenate([left[:half], left[half:] + down])
        else:
            right, left = right + up, left + down
        up = shift(right.astype(BF16), hidden, 1, ring).astype(F32)
        down = shift(left.astype(BF16), hidden, -1, ring).astype(F32)
    return wide[0] + up + down


def feature_part(weight, position, hidden, step, first=0, last=1, of=1):
    depth = hidden // RING
    part = weight.shape[0] // RING
    piece = part // of
    start = lax.rem(position // depth + step, RING) * part + first * piece
    rows = lax.dynamic_slice_in_dim(weight, start, (last - first) * piece, 0)
    return shift(rows, hidden, step, "across") if step else rows


def hold(values):
    return pltpu.with_memory_space_constraint(values, pltpu.HBM)


def whole_block():
    return pl.BlockSpec(memory_space=pltpu.VMEM)


def params(mib):
    return pltpu.CompilerParams(
        dimension_semantics=("arbitrary",), vmem_limit_bytes=mib * 1024 * 1024
    )


def silu_product(gate_value, up_value):
    return (gate_value / (1.0 + jnp.exp(-gate_value)) * up_value).astype(BF16)


def whole_gate_up(rows, gate, up):
    count, width = rows.shape
    units = gate.shape[1]
    pieces = 6
    depth = width // pieces

    def kernel(rows_hbm, gate_hbm, up_hbm, out_ref, rows_ref, gate_ref, up_ref, sems):
        copies = []
        for piece in range(pieces):
            features = pl.ds(piece * depth, depth)
            moved = [
                pltpu.make_async_copy(
                    rows_hbm.at[:, features], rows_ref.at[piece], sems.at[piece, 0]
                ),
                pltpu.make_async_copy(gate_hbm.at[features], gate_ref.at[piece], sems.at[piece, 1]),
                pltpu.make_async_copy(up_hbm.at[features], up_ref.at[piece], sems.at[piece, 2]),
            ]
            for copy in moved:
                copy.start()
            copies.append(moved)
        for copy in copies[0]:
            copy.wait()
        gate_sum = jnp.dot(rows_ref[0], gate_ref[0], preferred_element_type=F32)
        up_sum = jnp.dot(rows_ref[0], up_ref[0], preferred_element_type=F32)
        for piece in range(1, pieces):
            for copy in copies[piece]:
                copy.wait()
            gate_sum += jnp.dot(rows_ref[piece], gate_ref[piece], preferred_element_type=F32)
            up_sum += jnp.dot(rows_ref[piece], up_ref[piece], preferred_element_type=F32)
        out_ref[...] = silu_product(gate_sum, up_sum)

    anywhere = pl.BlockSpec(memory_space=pl.ANY)
    return pl.pallas_call(
        kernel,
        in_specs=[anywhere, anywhere, anywhere],
        out_specs=whole_block(),
        out_shape=jax.ShapeDtypeStruct((count, units), BF16),
        scratch_shapes=[
            pltpu.VMEM((pieces, count, depth), BF16),
            pltpu.VMEM((pieces, depth, units), BF16),
            pltpu.VMEM((pieces, depth, units), BF16),
            pltpu.SemaphoreType.DMA((pieces, 3)),
        ],
        compiler_params=pltpu.CompilerParams(vmem_limit_bytes=32 * 1024 * 1024),
        cost_estimate=pl.CostEstimate(
            flops=4 * count * width * units,
            bytes_accessed=2 * (count * width + 2 * width * units),
            transcendentals=count * units,
        ),
    )(hold(rows), hold(gate), hold(up))


def feature_blocks(weight):
    units, width = weight.shape
    part = width // RING

    def kernel(weight_hbm, out_ref, sems):
        moved = [
            pltpu.make_async_copy(
                weight_hbm.at[:, pl.ds(y * part, part)], out_ref.at[y], sems.at[y]
            )
            for y in range(RING)
        ]
        for copy in moved:
            copy.start()
        for copy in moved:
            copy.wait()

    return pl.pallas_call(
        kernel,
        in_specs=[pl.BlockSpec(memory_space=pl.ANY)],
        out_specs=whole_block(),
        out_shape=jax.ShapeDtypeStruct((RING, units, part), BF16),
        scratch_shapes=[pltpu.SemaphoreType.DMA((RING,))],
        compiler_params=pltpu.CompilerParams(vmem_limit_bytes=4 * 1024 * 1024),
        cost_estimate=pl.CostEstimate(
            flops=0, bytes_accessed=4 * units * width, transcendentals=0
        ),
    )(hold(weight))


def part_gate_up(rows, gate, up_parts, place):
    count, part = rows.shape
    units = gate.shape[1]

    def kernel(place_ref, rows_ref, gate_ref, up_ref, out_ref):
        block = rows_ref[...]
        out_ref[:, :units] = jnp.dot(block, gate_ref[...], preferred_element_type=F32).astype(BF16)
        up = up_ref[place_ref[0]]
        out_ref[:, units:] = jnp.dot(block, up, preferred_element_type=F32).astype(BF16)

    return pl.pallas_call(
        kernel,
        in_specs=[pl.BlockSpec(memory_space=pltpu.SMEM)] + [whole_block()] * 3,
        out_specs=whole_block(),
        out_shape=jax.ShapeDtypeStruct((count, 2 * units), BF16),
        compiler_params=pltpu.CompilerParams(vmem_limit_bytes=8 * 1024 * 1024),
        cost_estimate=pl.CostEstimate(
            flops=4 * count * part * units,
            bytes_accessed=2 * (count * part + 2 * part * units + count * units * 2),
            transcendentals=0,
        ),
    )(place, rows, gate, up_parts)


def down_product(gathered, down_parts, place, far):
    count, units = gathered[0].shape
    ring, _, part = down_parts.shape
    columns = part // 3

    def kernel(place_ref, *refs):
        rows, down_ref, out_ref = refs[:ring], refs[ring], refs[ring + 1]
        total = None
        for step in range(ring):
            source = lax.rem(place_ref[0] - step + ring, ring)
            product = jnp.dot(rows[step][...], down_ref[source], preferred_element_type=F32)
            total = product if total is None else total + product
        out_ref[...] = total.astype(BF16)

    return pl.pallas_call(
        kernel,
        grid=(part // columns,),
        in_specs=[pl.BlockSpec(memory_space=pltpu.SMEM)]
        + [whole_block()] * ring
        + [pl.BlockSpec((ring, units, columns), lambda n: (0, 0, n))],
        out_specs=pl.BlockSpec((count, columns), lambda n: (0, n)),
        out_shape=(pltpu.HBM if far else jax.ShapeDtypeStruct)((count, part), BF16),
        compiler_params=params(16),
        cost_estimate=pl.CostEstimate(
            flops=2 * count * part * units * ring,
            bytes_accessed=2 * (ring * count * units + ring * units * part + count * part),
            transcendentals=0,
        ),
    )(place, *gathered, down_parts)


def on_device(tokens, norm_gain, gate_weight, up_weight, down_weight, expert_ids, route_weight):
    experts = lax.axis_size("expert")
    hidden = lax.axis_size("hidden")
    depth = hidden // RING
    tok_count, width = tokens.shape
    part = width // RING
    units = gate_weight.shape[2]
    capacity = tok_count // 2
    slot_count = experts * capacity
    block = RING * slot_count
    across, along = row_groups(hidden)
    homes = home_groups(experts, hidden)
    both = ("expert", "hidden")

    position = lax.axis_index("hidden")
    own_ids = lax.dynamic_slice_in_dim(expert_ids, position * tok_count, tok_count, 0)
    own_weights = lax.dynamic_slice_in_dim(route_weight, position * tok_count, tok_count, 0)
    send, mix = routing(own_ids, own_weights, slot_count, capacity)

    def outgoing(state):
        normed = rms_norm(state, norm_gain)
        return jnp.einsum("ts,td->sd", send, normed, preferred_element_type=F32).astype(BF16)

    def finish(units_of, down_parts, far):
        gathered = [units_of] + [shift(units_of, hidden, k, "across") for k in (1, 2, 3)]
        return down_product(gathered, down_parts, (position // depth).reshape(1), far)

    def settle(summed, state):
        returned = exchange(summed.astype(BF16).reshape(experts * RING, capacity, part), both, homes)
        returned = returned.reshape(experts, RING, capacity, part).astype(F32)
        mixed = jnp.einsum(
            "tec,eycd->tyd",
            mix.reshape(tok_count, experts, capacity),
            returned,
            precision=lax.Precision.HIGHEST,
        ).reshape(tok_count, width)
        return (
            NUDGE * state.astype(F32) + NUDGE * (tokens.astype(F32) + mixed)
        ).astype(BF16)

    rows = outgoing(tokens).reshape(experts, 1, capacity, width)
    rows = jnp.broadcast_to(rows, (experts, RING, capacity, width))
    rows = exchange(rows.reshape(experts * RING, capacity, width), both, homes)
    rows = rows.reshape(block, width)
    gate, up, down = gate_weight[0], up_weight[0], down_weight[0]
    near = [feature_part(gate, position, hidden, step) for step in (1, 3)]
    near.append(feature_part(gate, position, hidden, 2, 0, 1, 2))
    gathered = lax.all_gather(rows, "hidden", axis=0, tiled=True, axis_index_groups=along)
    down_parts = exchange(feature_blocks(down), "hidden", across)
    gathered, near, down_parts = lax.optimization_barrier((gathered, near, down_parts))
    partial = finish(whole_gate_up(gathered, gate, up), down_parts, True)
    partial, up_in = lax.optimization_barrier((partial, up))
    up_parts = [feature_part(up_in, position, hidden, step) for step in range(RING)]
    summed = lax.psum_scatter(
        partial, "hidden", scatter_dimension=0, tiled=True, axis_index_groups=along
    )
    up_parts = exchange(up_in.reshape(RING, part, units), "hidden", across)
    summed, up_parts = lax.optimization_barrier((summed, up_parts))
    state = settle(summed, tokens)

    rows = outgoing(state).reshape(experts, capacity, RING, part).transpose(0, 2, 1, 3)
    rows = exchange(rows.reshape(experts * RING, capacity, part), both, homes)
    rows, gate_in = lax.optimization_barrier((rows, gate))
    far = feature_part(gate_in, position, hidden, 2, 1, 2, 2)
    blocks = ring_gather(rows.reshape(block, part), hidden)
    offsets = sorted(blocks)
    gathered = jnp.concatenate([blocks[step] for step in offsets])
    gathered, far = lax.optimization_barrier((gathered, far))
    own = feature_part(gate, position, hidden, 0)
    gate_parts = [own, near[0], jnp.concatenate([near[2], far]), near[1]]
    values = {
        step: part_gate_up(
            gathered,
            gate_parts[-step % RING],
            up_parts,
            lax.rem(position // depth + step + RING, RING).reshape(1),
        )
        for step in (2, 1, -1, 0)
    }
    values = ring_sum(values, 2, hidden, "across")
    partial = finish(silu_product(values[:, :units], values[:, units:]), down_parts, False)
    blocks = {
        step: partial[place * block : (place + 1) * block] for place, step in enumerate(offsets)
    }
    return settle(ring_sum(blocks, 4, hidden, "along"), state)


def solution(mesh):
    placed = (
        P(("expert", "hidden"), None),
        P(),
        P("expert", None, "hidden"),
        P("expert", None, "hidden"),
        P("expert", "hidden", None),
        P("expert", None),
        P("expert", None),
    )
    return jax.shard_map(
        on_device,
        mesh=mesh,
        in_specs=placed,
        out_specs=P(("expert", "hidden"), None),
        check_vma=False,
    )
```

```python
import jax
import jax.numpy as jnp
from jax import lax
from jax.experimental import pallas as pl
from jax.experimental.pallas import tpu as pltpu
from jax.sharding import PartitionSpec as P

ITERS = 2
EPSILON = 1e-05
NUDGE = 0.5
RING = 4

BF16 = jnp.bfloat16
F32 = jnp.float32


def row_groups(hidden):
    depth = hidden // RING
    across = [[y * depth + z for y in range(RING)] for z in range(depth)]
    along = [[y * depth + z for z in range(depth)] for y in range(RING)]
    return across, along


def home_groups(experts, hidden):
    depth = hidden // RING
    return [
        [e * hidden + y * depth + z for e in range(experts) for y in range(RING)]
        for z in range(depth)
    ]


def rms_norm(values, norm_gain):
    widened = values.astype(F32)
    mean_square = jnp.mean(widened * widened, axis=-1, keepdims=True)
    return (widened * lax.rsqrt(mean_square + EPSILON) * norm_gain).astype(BF16)


def routing(ids, weights, slot_count, capacity):
    tok_count = ids.shape[0]
    flat = ids.reshape(-1)
    order = jnp.arange(flat.shape[0], dtype=jnp.int32)
    earlier = (flat[:, None] == flat[None, :]) & (order[None, :] < order[:, None])
    within = jnp.sum(earlier.astype(jnp.int32), axis=1)
    slots = (flat * capacity + within).reshape(tok_count, 2)
    hits = slots[:, :, None] == jnp.arange(slot_count, dtype=jnp.int32)[None, None, :]
    send = jnp.sum(hits.astype(F32), axis=1).astype(BF16)
    mix = jnp.sum(jnp.where(hits, weights[:, :, None], 0.0), axis=1)
    return send, mix


def exchange(values, axis, groups):
    return lax.all_to_all(values, axis, 0, 0, tiled=True, axis_index_groups=groups)


def spread(values, copies, axis, groups):
    return exchange(jnp.broadcast_to(values[None], (copies,) + values.shape), axis, groups)


def shifts(hidden, step, ring):
    depth = hidden // RING
    if ring == "along":
        return [(i, (i // depth) * depth + (i % depth + step) % depth) for i in range(hidden)]
    return [(i, ((i // depth + step) % RING) * depth + i % depth) for i in range(hidden)]


def shift(values, hidden, step, ring):
    return lax.ppermute(values, "hidden", shifts(hidden, step, ring))


def ring_gather(own, hidden):
    half = own.shape[0] // 2
    up, down = own, own
    blocks = {0: own}
    for step in range(1, 4):
        up, down = shift(up, hidden, 1, "along"), shift(down, hidden, -1, "along")
        blocks[-step], blocks[step] = up, down
    blocks[4] = jnp.concatenate(
        [shift(up[:half], hidden, 1, "along"), shift(down[half:], hidden, -1, "along")]
    )
    return blocks


def ring_sum(blocks, far, hidden, ring):
    half = blocks[0].shape[0] // 2
    wide = {k: v.astype(F32) for k, v in blocks.items()}
    up = shift(blocks[far][:half], hidden, 1, ring).astype(F32)
    down = shift(blocks[far][half:], hidden, -1, ring).astype(F32)
    for step in range(far - 1, 0, -1):
        right, left = wide[step], wide[-step]
        if step == far - 1:
            right = jnp.concatenate([right[:half] + up, right[half:]])
            left = jnp.concatenate([left[:half], left[half:] + down])
        else:
            right, left = right + up, left + down
        up = shift(right.astype(BF16), hidden, 1, ring).astype(F32)
        down = shift(left.astype(BF16), hidden, -1, ring).astype(F32)
    return wide[0] + up + down


def feature_part(weight, position, hidden, step, first=0, last=1, of=1):
    depth = hidden // RING
    part = weight.shape[0] // RING
    piece = part // of
    start = lax.rem(position // depth + step, RING) * part + first * piece
    rows = lax.dynamic_slice_in_dim(weight, start, (last - first) * piece, 0)
    return shift(rows, hidden, step, "across") if step else rows


def hold(values):
    return pltpu.with_memory_space_constraint(values, pltpu.HBM)


def whole_block():
    return pl.BlockSpec(memory_space=pltpu.VMEM)


def params(mib):
    return pltpu.CompilerParams(
        dimension_semantics=("arbitrary",), vmem_limit_bytes=mib * 1024 * 1024
    )


def silu_product(gate_value, up_value):
    return (gate_value / (1.0 + jnp.exp(-gate_value)) * up_value).astype(BF16)


def whole_gate_up(rows, gate, up):
    count, width = rows.shape
    units = gate.shape[1]
    pieces = 6
    depth = width // pieces

    def kernel(rows_hbm, gate_hbm, up_hbm, out_ref, rows_ref, gate_ref, up_ref, sems):
        copies = []
        for piece in range(pieces):
            features = pl.ds(piece * depth, depth)
            moved = [
                pltpu.make_async_copy(
                    rows_hbm.at[:, features], rows_ref.at[piece], sems.at[piece, 0]
                ),
                pltpu.make_async_copy(gate_hbm.at[features], gate_ref.at[piece], sems.at[piece, 1]),
                pltpu.make_async_copy(up_hbm.at[features], up_ref.at[piece], sems.at[piece, 2]),
            ]
            for copy in moved:
                copy.start()
            copies.append(moved)
        for copy in copies[0]:
            copy.wait()
        gate_sum = jnp.dot(rows_ref[0], gate_ref[0], preferred_element_type=F32)
        up_sum = jnp.dot(rows_ref[0], up_ref[0], preferred_element_type=F32)
        for piece in range(1, pieces):
            for copy in copies[piece]:
                copy.wait()
            gate_sum += jnp.dot(rows_ref[piece], gate_ref[piece], preferred_element_type=F32)
            up_sum += jnp.dot(rows_ref[piece], up_ref[piece], preferred_element_type=F32)
        out_ref[...] = silu_product(gate_sum, up_sum)

    anywhere = pl.BlockSpec(memory_space=pl.ANY)
    return pl.pallas_call(
        kernel,
        in_specs=[anywhere, anywhere, anywhere],
        out_specs=whole_block(),
        out_shape=jax.ShapeDtypeStruct((count, units), BF16),
        scratch_shapes=[
            pltpu.VMEM((pieces, count, depth), BF16),
            pltpu.VMEM((pieces, depth, units), BF16),
            pltpu.VMEM((pieces, depth, units), BF16),
            pltpu.SemaphoreType.DMA((pieces, 3)),
        ],
        compiler_params=pltpu.CompilerParams(vmem_limit_bytes=32 * 1024 * 1024),
        cost_estimate=pl.CostEstimate(
            flops=4 * count * width * units,
            bytes_accessed=2 * (count * width + 2 * width * units),
            transcendentals=count * units,
        ),
    )(hold(rows), hold(gate), hold(up))


def feature_blocks(weight):
    units, width = weight.shape
    part = width // RING

    def kernel(weight_hbm, out_ref, sems):
        moved = [
            pltpu.make_async_copy(
                weight_hbm.at[:, pl.ds(y * part, part)], out_ref.at[y], sems.at[y]
            )
            for y in range(RING)
        ]
        for copy in moved:
            copy.start()
        for copy in moved:
            copy.wait()

    return pl.pallas_call(
        kernel,
        in_specs=[pl.BlockSpec(memory_space=pl.ANY)],
        out_specs=whole_block(),
        out_shape=jax.ShapeDtypeStruct((RING, units, part), BF16),
        scratch_shapes=[pltpu.SemaphoreType.DMA((RING,))],
        compiler_params=pltpu.CompilerParams(vmem_limit_bytes=4 * 1024 * 1024),
        cost_estimate=pl.CostEstimate(
            flops=0, bytes_accessed=4 * units * width, transcendentals=0
        ),
    )(hold(weight))


def part_gate_up(rows, gate, up_parts, place):
    count, part = rows.shape
    units = gate.shape[1]

    def kernel(place_ref, rows_ref, gate_ref, up_ref, out_ref):
        block = rows_ref[...]
        out_ref[:, :units] = jnp.dot(block, gate_ref[...], preferred_element_type=F32).astype(BF16)
        up = up_ref[place_ref[0]]
        out_ref[:, units:] = jnp.dot(block, up, preferred_element_type=F32).astype(BF16)

    return pl.pallas_call(
        kernel,
        in_specs=[pl.BlockSpec(memory_space=pltpu.SMEM)] + [whole_block()] * 3,
        grid=(1,),
        out_specs=pl.BlockSpec((count, 2 * units), lambda step: (0, 0)),
        out_shape=pltpu.HBM((count, 2 * units), BF16),
        compiler_params=pltpu.CompilerParams(vmem_limit_bytes=8 * 1024 * 1024),
        cost_estimate=pl.CostEstimate(
            flops=4 * count * part * units,
            bytes_accessed=2 * (count * part + 2 * part * units + count * units * 2),
            transcendentals=0,
        ),
    )(place, rows, gate, up_parts)


def down_product(gathered, down_parts, place, far):
    count, units = gathered[0].shape
    ring, _, part = down_parts.shape
    columns = part // 3

    def kernel(place_ref, *refs):
        rows, down_ref, out_ref = refs[:ring], refs[ring], refs[ring + 1]
        total = None
        for step in range(ring):
            source = lax.rem(place_ref[0] - step + ring, ring)
            product = jnp.dot(rows[step][...], down_ref[source], preferred_element_type=F32)
            total = product if total is None else total + product
        out_ref[...] = total.astype(BF16)

    return pl.pallas_call(
        kernel,
        grid=(part // columns,),
        in_specs=[pl.BlockSpec(memory_space=pltpu.SMEM)]
        + [whole_block()] * ring
        + [pl.BlockSpec((ring, units, columns), lambda n: (0, 0, n))],
        out_specs=pl.BlockSpec((count, columns), lambda n: (0, n)),
        out_shape=(pltpu.HBM if far else jax.ShapeDtypeStruct)((count, part), BF16),
        compiler_params=params(16),
        cost_estimate=pl.CostEstimate(
            flops=2 * count * part * units * ring,
            bytes_accessed=2 * (ring * count * units + ring * units * part + count * part),
            transcendentals=0,
        ),
    )(place, *gathered, down_parts)


def on_device(tokens, norm_gain, gate_weight, up_weight, down_weight, expert_ids, route_weight):
    experts = lax.axis_size("expert")
    hidden = lax.axis_size("hidden")
    depth = hidden // RING
    tok_count, width = tokens.shape
    part = width // RING
    units = gate_weight.shape[2]
    capacity = tok_count // 2
    slot_count = experts * capacity
    block = RING * slot_count
    across, along = row_groups(hidden)
    homes = home_groups(experts, hidden)
    both = ("expert", "hidden")

    position = lax.axis_index("hidden")
    own_ids = lax.dynamic_slice_in_dim(expert_ids, position * tok_count, tok_count, 0)
    own_weights = lax.dynamic_slice_in_dim(route_weight, position * tok_count, tok_count, 0)
    send, mix = routing(own_ids, own_weights, slot_count, capacity)

    def outgoing(state):
        normed = rms_norm(state, norm_gain)
        return jnp.einsum("ts,td->sd", send, normed, preferred_element_type=F32).astype(BF16)

    def finish(units_of, down_parts, far):
        gathered = [units_of] + [shift(units_of, hidden, k, "across") for k in (1, 2, 3)]
        return down_product(gathered, down_parts, (position // depth).reshape(1), far)

    def settle(summed, state):
        returned = exchange(summed.astype(BF16).reshape(experts * RING, capacity, part), both, homes)
        returned = returned.reshape(experts, RING, capacity, part).astype(F32)
        mixed = jnp.einsum(
            "tec,eycd->tyd",
            mix.reshape(tok_count, experts, capacity),
            returned,
            precision=lax.Precision.HIGHEST,
        ).reshape(tok_count, width)
        return (
            NUDGE * state.astype(F32) + NUDGE * (tokens.astype(F32) + mixed)
        ).astype(BF16)

    rows = outgoing(tokens).reshape(experts, 1, capacity, width)
    rows = jnp.broadcast_to(rows, (experts, RING, capacity, width))
    rows = exchange(rows.reshape(experts * RING, capacity, width), both, homes)
    rows = rows.reshape(block, width)
    gate, up, down = gate_weight[0], up_weight[0], down_weight[0]
    near = [feature_part(gate, position, hidden, step) for step in (1, 3)]
    near.append(feature_part(gate, position, hidden, 2, 0, 1, 2))
    gathered = lax.all_gather(rows, "hidden", axis=0, tiled=True, axis_index_groups=along)
    down_parts = exchange(feature_blocks(down), "hidden", across)
    gathered, near, down_parts = lax.optimization_barrier((gathered, near, down_parts))
    partial = finish(whole_gate_up(gathered, gate, up), down_parts, True)
    partial, up_in = lax.optimization_barrier((partial, up))
    up_parts = [feature_part(up_in, position, hidden, step) for step in range(RING)]
    summed = lax.psum_scatter(
        partial, "hidden", scatter_dimension=0, tiled=True, axis_index_groups=along
    )
    up_parts = exchange(up_in.reshape(RING, part, units), "hidden", across)
    summed, up_parts = lax.optimization_barrier((summed, up_parts))
    state = settle(summed, tokens)

    rows = outgoing(state).reshape(experts, capacity, RING, part).transpose(0, 2, 1, 3)
    rows = exchange(rows.reshape(experts * RING, capacity, part), both, homes)
    rows, gate_in = lax.optimization_barrier((rows, gate))
    far = feature_part(gate_in, position, hidden, 2, 1, 2, 2)
    blocks = ring_gather(rows.reshape(block, part), hidden)
    offsets = sorted(blocks)
    gathered = jnp.concatenate([blocks[step] for step in offsets])
    gathered, far = lax.optimization_barrier((gathered, far))
    own = feature_part(gate, position, hidden, 0)
    gate_parts = [own, near[0], jnp.concatenate([near[2], far]), near[1]]
    values = {
        step: part_gate_up(
            gathered,
            gate_parts[-step % RING],
            up_parts,
            lax.rem(position // depth + step + RING, RING).reshape(1),
        )
        for step in (2, 1, -1, 0)
    }
    values = ring_sum(values, 2, hidden, "across")
    partial = finish(silu_product(values[:, :units], values[:, units:]), down_parts, False)
    blocks = {
        step: partial[place * block : (place + 1) * block] for place, step in enumerate(offsets)
    }
    return settle(ring_sum(blocks, 4, hidden, "along"), state)


def solution(mesh):
    placed = (
        P(("expert", "hidden"), None),
        P(),
        P("expert", None, "hidden"),
        P("expert", None, "hidden"),
        P("expert", "hidden", None),
        P("expert", None),
        P("expert", None),
    )
    return jax.shard_map(
        on_device,
        mesh=mesh,
        in_specs=placed,
        out_specs=P(("expert", "hidden"), None),
        check_vma=False,
    )
```
